256 devices in a mesh: gx: 128 (over x, z, y), gy: 2 (over core).
Axes of the slice: x: 4, y: 4, z: 8, core: 2. Of those that a mesh axis runs over, the one named last changes fastest.
Arguments:
- records: float32 [786432, 128], P('gx', 'gy'), may hold values from -1.8 to 1.8
- idents: float32 [524288, 128], P('gx', 'gy'), may hold values from -1.8 to 1.8
- rec_count: int32 [786432], P('gx'), may hold values from 1 to 1000
- id_count: int32 [524288], P('gx'), may hold values from 1 to 1000
- observed: bfloat16 [24576, 128, 128], P('gx'), may hold values from -6 to 6
- send_list: int32 [16384, 1], P('gx'), may hold values from 0 to 47
- slot_of_block: int32 [24576], P('gx'), may hold values from 0 to 127, as said below
- id_of_block: int32 [24576], P('gx'), may hold values from 0 to 31
Outputs:
- new_records: float32 [786432, 128], P('gx', 'gy')
- new_idents: float32 [524288, 128], P('gx', 'gy')
The draws below stay inside these ranges and needn't reach their ends.
Inputs may be any that keep to these rules, and one draw needn't show every extreme that they name: `slot_of_block`: each owner's 192 entries use every slot from 0 to 127.
All inputs are finite; a program needn't handle non-finite values.
Results may differ from the reference program's by a relative error of at most 0.013.
Values may be sent and summed in bfloat16 or wider, within the bound.
No kernel may reach another device: no remote copies, remote signals or barrier semaphores. Data moves between devices by JAX's collectives and lax.ppermute only.
A program may use at most 128 MiB of HBM per device.

```python
import jax
import jax.numpy as jnp
from jax import lax

RANK = 128
BLK = 128
RB_DEV = 48
IB_DEV = 32
NB_DEV = 192
SLOTS = 1
RECORDS = 786432
IDENTS = 524288
NB_ALL = 24576
PAIRS = 16384
N_GX = 128


def draw_slot_of_block(key, part):
    total_slots = N_GX * SLOTS
    row_keys = jax.random.split(jax.random.fold_in(key, 11), N_GX)
    covered = jax.vmap(lambda single: jax.random.permutation(single, total_slots))(row_keys).astype(jnp.int32)
    others = jax.random.randint(jax.random.fold_in(key, 13), (N_GX, NB_DEV - total_slots), 0, total_slots).astype(jnp.int32)
    joined = jnp.concatenate([covered, others], axis=1)
    order_keys = jax.random.split(jax.random.fold_in(key, 17), N_GX)
    orders = jax.vmap(lambda single: jax.random.permutation(single, NB_DEV))(order_keys)
    shuffled = jnp.take_along_axis(joined, orders, axis=1)
    return shuffled.reshape(-1).astype(jnp.int32)


def touch_ends(values, own_key, low, high):
    longest = values.shape.index(max(values.shape))
    spots = []
    for shift in (0, 1):
        where = [jax.random.randint(jax.random.fold_in(own_key, axis), (), 0, length) for axis, length in enumerate(values.shape)]
        where[longest] = (where[longest] + shift) % values.shape[longest]
        spots.append(tuple(where))
    return values.at[spots[0]].set(low).at[spots[1]].set(high)


def block_scale(rng, extent, cuts, low, largest):
    def one(axis_at, shards_of):
        steps = jax.random.uniform(jax.random.fold_in(jax.random.fold_in(rng, 6), axis_at), (shards_of,), jnp.float32, low / len(cuts), largest / len(cuts))
        return jnp.repeat(jnp.exp(steps), extent[axis_at] // shards_of).reshape((-1,) + (1,) * (len(extent) - axis_at - 1))

    loudness = one(*cuts[0])
    for cut in cuts[1:]:
        loudness = loudness * one(*cut)
    return loudness


def noise(own_key, dims, scale, bound, shards=(), kind=jnp.bfloat16):
    drawn = jax.random.normal(own_key, dims, jnp.float32) * scale
    if len(shards) > 0:
        drawn = block_scale(own_key, dims, shards, -0.22, 0.18) * drawn
    return jnp.clip(drawn, min=-bound, max=bound).astype(kind)


def setup_inputs(seed: int = 0) -> dict:
    streams_of = jax.random.split(jax.random.key(seed), 9)
    return {
        "records": noise(streams_of[0], (RECORDS, RANK), 0.3, 1.8, ((0, 128), (1, 2)), jnp.float32),
        "idents": noise(streams_of[1], (IDENTS, RANK), 0.3, 1.8, ((0, 128), (1, 2)), jnp.float32),
        "rec_count": touch_ends(jax.random.randint(streams_of[2], (RECORDS,), 1, 1001), jax.random.fold_in(streams_of[2], 1), 1, 1000).astype(jnp.int32),
        "id_count": touch_ends(jax.random.randint(streams_of[3], (IDENTS,), 1, 1001), jax.random.fold_in(streams_of[3], 1), 1, 1000).astype(jnp.int32),
        "observed": noise(streams_of[4], (NB_ALL, BLK, BLK), 1.0, 6.0, ((0, 128),)),
        "send_list": touch_ends(jax.random.randint(streams_of[5], (PAIRS, SLOTS), 0, RB_DEV), jax.random.fold_in(streams_of[5], 1), 0, RB_DEV - 1).astype(jnp.int32),
        "slot_of_block": draw_slot_of_block(jax.random.fold_in(streams_of[8], 71), 0),
        "id_of_block": touch_ends(jax.random.randint(streams_of[7], (NB_ALL,), 0, IB_DEV), jax.random.fold_in(streams_of[7], 1), 0, IB_DEV - 1).astype(jnp.int32),
    }


def reference(records, idents, rec_count, id_count, observed, send_list, slot_of_block, id_of_block):
    half_cols = RANK // 2
    rec_bf = records.astype(jnp.bfloat16).reshape(N_GX * RB_DEV, BLK, RANK)
    id_bf = idents.astype(jnp.bfloat16).reshape(N_GX * IB_DEV, BLK, RANK)
    rec_weight = (jnp.log1p(rec_count.astype(jnp.float32)) / jnp.log(jnp.float32(1001.0))).astype(jnp.bfloat16)
    rec_weight = rec_weight.astype(jnp.float32).reshape(N_GX * RB_DEV, BLK)
    id_weight = (jnp.log1p(id_count.astype(jnp.float32)) / jnp.log(jnp.float32(1001.0))).reshape(N_GX * IB_DEV, BLK)
    owner = (jnp.arange(N_GX * NB_DEV) // NB_DEV).astype(jnp.int32)
    source = (slot_of_block // SLOTS).astype(jnp.int32)
    position = (slot_of_block % SLOTS).astype(jnp.int32)
    rec_block = (source * RB_DEV + send_list[source * N_GX + owner, position]).astype(jnp.int32)
    id_block = (owner * IB_DEV + id_of_block).astype(jnp.int32)

    def block_step(rec_grad, device):
        start = (device * NB_DEV).astype(jnp.int32)
        my_rec = lax.dynamic_slice_in_dim(rec_block, start, NB_DEV)
        my_id = lax.dynamic_slice_in_dim(id_block, start, NB_DEV)
        my_local = lax.dynamic_slice_in_dim(id_of_block, start, NB_DEV).astype(jnp.int32)
        my_obs = lax.dynamic_slice_in_dim(observed, start, NB_DEV, 0).astype(jnp.float32)
        left_rows = rec_bf[my_rec].astype(jnp.float32)
        right_rows = id_bf[my_id].astype(jnp.float32)
        part_low = jnp.einsum("bik,bjk->bij", left_rows[:, :, :half_cols], right_rows[:, :, :half_cols]).astype(jnp.bfloat16)
        part_high = jnp.einsum("bik,bjk->bij", left_rows[:, :, half_cols:], right_rows[:, :, half_cols:]).astype(jnp.bfloat16)
        weight_grid = rec_weight[my_rec][:, :, None] * id_weight[my_id][:, None, :]
        summed = part_low.astype(jnp.float32) + part_high.astype(jnp.float32)
        resid = (weight_grid * (summed - my_obs)).astype(jnp.bfloat16).astype(jnp.float32)
        grad_left = jnp.einsum("bij,bjk->bik", resid, right_rows)
        grad_right = jnp.einsum("bij,bik->bjk", resid, left_rows)
        rec_grad = rec_grad.at[my_rec].add(grad_left)
        id_part = jnp.zeros((IB_DEV, BLK, RANK), jnp.float32).at[my_local].add(grad_right)
        return rec_grad, id_part

    start_grad = jnp.zeros((N_GX * RB_DEV, BLK, RANK), jnp.float32)
    rec_grad, id_grad = lax.scan(block_step, start_grad, jnp.arange(N_GX, dtype=jnp.int32))
    rec_grad = rec_grad.reshape(records.shape)
    id_grad = id_grad.reshape(idents.shape)
    new_records = records - 0.05 * (rec_grad + 0.1 * records)
    new_idents = idents - 0.05 * (id_grad + 0.1 * idents)
    return new_records, new_idents
```

```python
import functools

import jax
import jax.numpy as jnp
from jax import lax
from jax.experimental import pallas as pl
from jax.experimental.pallas import tpu as pltpu
from jax.sharding import PartitionSpec as P

F32, BF16 = jnp.float32, jnp.bfloat16
STEP = 0.05
DECAY = 0.1
VMEM = pl.BlockSpec(memory_space=pltpu.VMEM)
SMEM = pl.BlockSpec(memory_space=pltpu.SMEM)
PARAMS = pltpu.CompilerParams(vmem_limit_bytes=48 << 20)


def count_weight(count):
    return jnp.log(1.0 + count.astype(F32)) / jnp.log(F32(1001.0))


def low_lanes(half):
    lane = lax.broadcasted_iota(jnp.int32, (1, 2 * half), 1)
    return lane < half


def split_kernel(core_ref, rec_ref, id_ref, keep_ref, send_ref, id_out_ref):
    core = core_ref[0]
    pairs, _, blk = keep_ref.shape
    low = low_lanes(blk // 2)

    def pair(m, _):
        first = rec_ref[:, pl.ds(pl.multiple_of(m * 2 * blk, blk), blk)]
        second = rec_ref[:, pl.ds(pl.multiple_of(m * 2 * blk + blk, blk), blk)]
        half0 = jnp.where(low, first, pltpu.roll(second, blk // 2, 1))
        half1 = jnp.where(low, pltpu.roll(first, blk // 2, 1), second)
        keep_ref[m] = jnp.where(core == 0, half0, half1).astype(BF16)
        send_ref[m] = jnp.where(core == 0, half1, half0).astype(BF16)
        return 0

    lax.fori_loop(0, pairs, pair, 0, unroll=2)
    for n in range(id_out_ref.shape[0]):
        id_out_ref[n] = id_ref[:, n * blk : (n + 1) * blk].astype(BF16)


def pack_kernel(core_ref, list_ref, keep_ref, recv_ref, count_ref, out_ref, weight_ref, blocks, weights):
    core = core_ref[0]
    pairs, half_cols, blk = keep_ref.shape
    half = blk // 2

    def pair(m, _):
        keep, recv = keep_ref[m].astype(F32), recv_ref[m].astype(F32)
        low = jnp.where(core == 0, keep, recv)
        high = jnp.where(core == 0, recv, keep)
        rows = jnp.concatenate([low, high], axis=0).T.astype(BF16)
        blocks[2 * m] = rows[:half]
        blocks[2 * m + 1] = rows[half:]
        return 0

    lax.fori_loop(0, pairs, pair, 0, unroll=2)
    weight = count_weight(count_ref[...])
    weights[...] = jnp.where(core == 0, weight, pltpu.roll(weight, half, 1))

    def chunk(e, _):
        r = list_ref[e]
        out_ref[e] = blocks[r]
        weight_ref[pl.ds(e, 1), :] = weights[pl.ds(r, 1), :]
        return 0

    lax.fori_loop(0, out_ref.shape[0], chunk, 0, unroll=8)


def ident_kernel(core_ref, own_ref, peer_ref, count_ref, idt_ref, id_ref, weight_ref):
    core = core_ref[0]

    def block(n, _):
        own, peer = own_ref[n].astype(F32), peer_ref[n].astype(F32)
        low = jnp.where(core == 0, own, peer)
        high = jnp.where(core == 0, peer, own)
        full = jnp.concatenate([low, high], axis=0)
        idt_ref[n] = full.astype(BF16)
        id_ref[n] = full.T.astype(BF16)
        return 0

    lax.fori_loop(0, own_ref.shape[0], block, 0, unroll=2)
    weight_ref[...] = count_weight(count_ref[...])


def score_kernel(
    core_ref, slot_ref, ident_ref, rows_ref, idt_ref, id_ref, weight_ref, obs_ref, resid_ref, out_ref, grad
):
    step = pl.program_id(0)
    group = obs_ref.shape[0]

    @pl.when(step == 0)
    def _():
        grad[...] = jnp.zeros_like(grad)

    parts = []
    for u in range(group):
        b = step * group + u
        s, n = slot_ref[b], ident_ref[b]
        score = jnp.dot(rows_ref[s], idt_ref[n], preferred_element_type=F32)
        resid = (weight_ref[pl.ds(n, 1), :] * (score - obs_ref[u].astype(F32))).astype(BF16)
        resid_ref[u] = resid
        parts.append((s, jnp.dot(resid, id_ref[n], preferred_element_type=F32)))
    for s, part in parts:
        grad[s] += part

    @pl.when(step == pl.num_programs(0) - 1)
    def _():
        out_ref[...] = grad[...].astype(BF16)


def ident_grad_kernel(core_ref, slot_ref, ident_ref, rows_ref, weight_ref, resid_ref, keep_ref, send_ref, grad, turned):
    step = pl.program_id(0)
    group = resid_ref.shape[0]
    half = resid_ref.shape[1]
    core = core_ref[0]

    @pl.when(step == 0)
    def _():
        grad[...] = jnp.zeros_like(grad)

        def turn(s, _):
            rows = rows_ref[s].astype(F32).T
            turned[s] = (rows * weight_ref[pl.ds(s, 1), :half]).astype(BF16)
            return 0

        lax.fori_loop(0, rows_ref.shape[0], turn, 0, unroll=4)

    parts = []
    for u in range(group):
        b = step * group + u
        s, n = slot_ref[b], ident_ref[b]
        parts.append((n, jnp.dot(turned[s], resid_ref[u], preferred_element_type=F32)))
    for n, part in parts:
        grad[n] += part

    @pl.when(step == pl.num_programs(0) - 1)
    def _():
        for n in range(grad.shape[0]):
            own = pl.multiple_of(core * half, half)
            other = pl.multiple_of((1 - core) * half, half)
            keep_ref[n] = grad[n, pl.ds(own, half), :]
            send_ref[n] = grad[n, pl.ds(other, half), :]


def ident_update_kernel(id_ref, own_ref, peer_ref, out_ref):
    blk = own_ref.shape[2]
    for n in range(own_ref.shape[0]):
        old = id_ref[:, n * blk : (n + 1) * blk]
        grad = own_ref[n] + peer_ref[n]
        out_ref[:, n * blk : (n + 1) * blk] = old - STEP * (grad + DECAY * old)


def collect_kernel(core_ref, list_ref, back_ref, count_ref, keep_ref, send_ref, grad, weights):
    core = core_ref[0]
    pairs, half_cols, blk = keep_ref.shape
    half = blk // 2
    grad[...] = jnp.zeros_like(grad)
    weight = count_weight(count_ref[...]).astype(BF16).astype(F32)
    weights[...] = jnp.where(core == 0, weight, pltpu.roll(weight, half, 1))

    def add(e, _):
        r = list_ref[e]
        grad[r] += back_ref[e].astype(F32)
        return 0

    lax.fori_loop(0, back_ref.shape[0], add, 0, unroll=8)
    low = low_lanes(half)

    def pair(m, _):
        both = jnp.concatenate([grad[2 * m], grad[2 * m + 1]], axis=0).T
        row = jnp.where(low, weights[pl.ds(2 * m, 1), :], pltpu.roll(weights[pl.ds(2 * m + 1, 1), :], half, 1))
        both = both * row
        first, last = both[:half_cols], both[half_cols:]
        keep_ref[m] = jnp.where(core == 0, first, last)
        send_ref[m] = jnp.where(core == 0, last, first)
        return 0

    lax.fori_loop(0, pairs, pair, 0, unroll=2)


def record_update_kernel(core_ref, rec_ref, keep_ref, recv_ref, out_ref):
    core = core_ref[0]
    pairs, _, blk = keep_ref.shape
    low = low_lanes(blk // 2)

    def pair(m, _):
        keep, recv = keep_ref[m], recv_ref[m]
        half0 = jnp.where(core == 0, keep, recv)
        half1 = jnp.where(core == 0, recv, keep)
        grads = (
            jnp.where(low, half0, pltpu.roll(half1, blk // 2, 1)),
            jnp.where(low, pltpu.roll(half0, blk // 2, 1), half1),
        )
        for k, grad in enumerate(grads):
            at = pl.ds(pl.multiple_of(m * 2 * blk + k * blk, blk), blk)
            old = rec_ref[:, at]
            out_ref[:, at] = old - STEP * (grad + DECAY * old)
        return 0

    lax.fori_loop(0, pairs, pair, 0, unroll=2)


def call(kernel, outs, ins, scratch=(), name=None):
    return pl.pallas_call(
        kernel,
        out_shape=[jax.ShapeDtypeStruct(s, t) for s, t in outs],
        in_specs=ins,
        out_specs=[VMEM] * len(outs),
        scratch_shapes=[pltpu.VMEM(s, t) for s, t in scratch],
        compiler_params=PARAMS,
        name=name,
    )


def body(records, idents, rec_count, id_count, observed, send_list, slot_of_block, id_of_block):
    peers = lax.axis_size("gx")
    core = lax.axis_index("gy").astype(jnp.int32).reshape(1)
    blocks, blk = observed.shape[0], observed.shape[1]
    half_cols = records.shape[1]
    rank = 2 * half_cols
    half = blk // 2
    recs, ids = records.shape[0] // blk, idents.shape[0] // blk
    pairs = recs // 2
    rec_t, id_t = records.T, idents.T
    sends = send_list.reshape(-1)
    rec_count, id_count = rec_count.reshape(recs, blk), id_count.reshape(ids, blk)
    swap = functools.partial(lax.ppermute, axis_name="gy", perm=[(0, 1), (1, 0)])
    exchange = functools.partial(lax.all_to_all, axis_name="gx", split_axis=0, concat_axis=0, tiled=True)

    half_shape = (pairs, half_cols, blk)
    keep, send, id_half = call(
        split_kernel,
        [(half_shape, BF16), (half_shape, BF16), ((ids, half_cols, blk), BF16)],
        [SMEM, VMEM, VMEM],
        name="split",
    )(core, rec_t, id_t)
    recv = swap(send)
    chunks, chunk_weight = call(
        pack_kernel,
        [((peers, half, rank), BF16), ((peers, blk), F32)],
        [SMEM, SMEM, VMEM, VMEM, VMEM],
        [((recs, half, rank), BF16), ((recs, blk), F32)],
        name="pack",
    )(core, sends, keep, recv, rec_count)
    arrived_weight = exchange(chunk_weight.astype(BF16).reshape(peers, 1, blk)).reshape(peers, blk).astype(F32)
    arrived = exchange(chunks)

    id_peer = swap(id_half)
    idt, id_rows, id_weight = call(
        ident_kernel,
        [((ids, rank, blk), BF16), ((ids, blk, rank), BF16), ((ids, blk), F32)],
        [SMEM, VMEM, VMEM, VMEM],
        name="ident",
    )(core, id_half, id_peer, id_count)

    group = 8

    def whole(shape):
        return pl.BlockSpec(shape, lambda *_: (0,) * len(shape))

    resid, slot_grad = pl.pallas_call(
        score_kernel,
        out_shape=[
            jax.ShapeDtypeStruct((blocks, half, blk), BF16),
            jax.ShapeDtypeStruct((peers, half, rank), BF16),
        ],
        grid_spec=pltpu.PrefetchScalarGridSpec(
            num_scalar_prefetch=3,
            grid=(blocks // group,),
            in_specs=[
                whole((peers, half, rank)),
                whole((ids, rank, blk)),
                whole((ids, blk, rank)),
                whole((ids, blk)),
                pl.BlockSpec((group, half, blk), lambda i, core, *_: (i, core[0], 0)),
            ],
            out_specs=[pl.BlockSpec((group, half, blk), lambda i, *_: (i, 0, 0)), whole((peers, half, rank))],
            scratch_shapes=[pltpu.VMEM((peers, half, rank), F32)],
        ),
        compiler_params=PARAMS,
        name="score",
    )(core, slot_of_block, id_of_block, arrived, idt, id_rows, id_weight, observed)
    returned = exchange(slot_grad)

    id_keep, id_send = pl.pallas_call(
        ident_grad_kernel,
        out_shape=[jax.ShapeDtypeStruct((ids, half_cols, blk), F32)] * 2,
        grid_spec=pltpu.PrefetchScalarGridSpec(
            num_scalar_prefetch=3,
            grid=(blocks // group,),
            in_specs=[
                whole((peers, half, rank)),
                whole((peers, blk)),
                pl.BlockSpec((group, half, blk), lambda i, *_: (i, 0, 0)),
            ],
            out_specs=[whole((ids, half_cols, blk))] * 2,
            scratch_shapes=[pltpu.VMEM((ids, rank, blk), F32), pltpu.VMEM((peers, rank, half), BF16)],
        ),
        compiler_params=PARAMS,
        name="ident_grad",
    )(core, slot_of_block, id_of_block, arrived, arrived_weight, resid)
    id_recv = swap(id_send)
    (new_id_t,) = call(ident_update_kernel, [(id_t.shape, F32)], [VMEM] * 3, name="ident_update")(
        id_t, id_keep, id_recv
    )

    rec_keep, rec_send = call(
        collect_kernel,
        [(half_shape, F32), (half_shape, F32)],
        [SMEM, SMEM, VMEM, VMEM],
        [((recs, half, rank), F32), ((recs, blk), F32)],
        name="collect",
    )(core, sends, returned, rec_count)
    rec_recv = swap(rec_send)
    (new_rec_t,) = call(record_update_kernel, [(rec_t.shape, F32)], [SMEM, VMEM, VMEM, VMEM], name="record_update")(
        core, rec_t, rec_keep, rec_recv
    )
    return new_rec_t.T, new_id_t.T


def solution(mesh):
    in_specs = (
        P("gx", "gy"),
        P("gx", "gy"),
        P("gx"),
        P("gx"),
        P("gx", None, None),
        P("gx", None),
        P("gx"),
        P("gx"),
    )
    out_specs = (P("gx", "gy"), P("gx", "gy"))
    return jax.shard_map(body, mesh=mesh, in_specs=in_specs, out_specs=out_specs, check_vma=False)
```

```python
import functools

import jax
import jax.numpy as jnp
from jax import lax
from jax.experimental import pallas as pl
from jax.experimental.pallas import tpu as pltpu
from jax.sharding import PartitionSpec as P

F32, BF16 = jnp.float32, jnp.bfloat16
STEP = 0.05
DECAY = 0.1
VMEM = pl.BlockSpec(memory_space=pltpu.VMEM)
SMEM = pl.BlockSpec(memory_space=pltpu.SMEM)
HBM = pl.BlockSpec(memory_space=pltpu.HBM)
GRID = (4, 8, 4)
PARAMS = pltpu.CompilerParams(vmem_limit_bytes=24 << 20)


def count_weight(count):
    return jnp.log(1.0 + count.astype(F32)) / jnp.log(F32(1001.0))


def low_lanes(half):
    lane = lax.broadcasted_iota(jnp.int32, (1, 2 * half), 1)
    return lane < half


def split_kernel(core_ref, rec_ref, keep_ref, send_ref, rows, sems):
    core = core_ref[0]
    pairs, _, blk = keep_ref.shape
    low = low_lanes(blk // 2)
    parts = sems.shape[0]
    width = rec_ref.shape[1] // parts

    def copy(p):
        at = pl.ds(p * width, width)
        return pltpu.make_async_copy(rec_ref.at[:, at], rows.at[:, at], sems.at[p])

    for p in range(parts):
        copy(p).start()
    for m in range(pairs):
        if m % (pairs // parts) == 0:
            copy(m // (pairs // parts)).wait()
        first = rows[:, 2 * m * blk : (2 * m + 1) * blk]
        second = rows[:, (2 * m + 1) * blk : (2 * m + 2) * blk]
        half0 = jnp.where(low, first, pltpu.roll(second, blk // 2, 1))
        half1 = jnp.where(low, pltpu.roll(first, blk // 2, 1), second)
        keep_ref[m] = jnp.where(core == 0, half0, half1).astype(BF16)
        send_ref[m] = jnp.where(core == 0, half1, half0).astype(BF16)


def cast_kernel(id_ref, out_ref):
    blk = out_ref.shape[2]
    for n in range(out_ref.shape[0]):
        out_ref[n] = id_ref[:, n * blk : (n + 1) * blk].astype(BF16)


def pack_kernel(core_ref, list_ref, keep_ref, recv_ref, out_ref, blocks, chunks, sems):
    core = core_ref[0]
    pairs, half_cols, blk = keep_ref.shape
    half = blk // 2

    def pair(m, _):
        keep, recv = keep_ref[m].astype(F32), recv_ref[m].astype(F32)
        low = jnp.where(core == 0, keep, recv)
        high = jnp.where(core == 0, recv, keep)
        rows = jnp.concatenate([low, high], axis=0).T.astype(BF16)
        blocks[2 * m] = rows[:half]
        blocks[2 * m + 1] = rows[half:]
        return 0

    lax.fori_loop(0, pairs, pair, 0, unroll=4)

    def chunk(e, _):
        chunks[e] = blocks[list_ref[e]]
        return 0

    store_parts(chunks, out_ref, sems, lambda first, count: lax.fori_loop(first, first + count, chunk, 0, unroll=8))


def store_parts(scratch, out_ref, sems, fill):
    parts = sems.shape[0]
    count = scratch.shape[0] // parts
    copies = []
    for p in range(parts):
        fill(p * count, count)
        at = pl.ds(p * count, count)
        copies.append(pltpu.make_async_copy(scratch.at[at], out_ref.at[at], sems.at[p]))
        copies[-1].start()
    for copy in copies:
        copy.wait()


def weigh_kernel(core_ref, chip_ref, list_ref, count_ref, out_ref, weights):
    core = core_ref[0]
    peers, blk = out_ref.shape
    weight = count_weight(count_ref[...]).astype(BF16).astype(F32)
    weights[...] = jnp.where(core == 0, weight, pltpu.roll(weight, blk // 2, 1))

    def row(d, _):
        out_ref[pl.ds(d, 1), :] = weights[pl.ds(list_ref[combine(chip_ref[0], d, 1)], 1), :]
        return 0

    lax.fori_loop(0, peers, row, 0, unroll=8)


def coords(chip):
    n0, n1, n2 = GRID
    return lax.div(chip, n1 * n2), lax.rem(lax.div(chip, n2), n1), lax.rem(chip, n2)


def combine(chip, other, sign):
    x, y, z = (lax.rem(a + sign * b + n, n) for a, b, n in zip(coords(chip), coords(other), GRID))
    return (x * GRID[1] + y) * GRID[2] + z


def ident_kernel(core_ref, own_ref, peer_ref, count_ref, idt_ref, id_ref, weight_ref):
    core = core_ref[0]

    def block(n, _):
        own, peer = own_ref[n].astype(F32), peer_ref[n].astype(F32)
        low = jnp.where(core == 0, own, peer)
        high = jnp.where(core == 0, peer, own)
        full = jnp.concatenate([low, high], axis=0)
        idt_ref[n] = full.astype(BF16)
        id_ref[n] = full.T.astype(BF16)
        return 0

    lax.fori_loop(0, own_ref.shape[0], block, 0, unroll=2)
    weight_ref[...] = count_weight(count_ref[...])


GROUP = 16


def score_kernel(
    core_ref,
    slot_ref,
    ident_ref,
    rows_ref,
    weight_ref,
    idt_hbm,
    id_hbm,
    obs_hbm,
    resid_hbm,
    out_hbm,
    idt_ref,
    id_ref,
    obs_ref,
    resid_ref,
    grad,
    chunks,
    sems,
    in_sems,
    resid_sems,
    out_sems,
):
    blocks, half, _ = obs_ref.shape
    groups = blocks // GROUP
    rows_at = pl.ds(pl.multiple_of(core_ref[0] * half, half), half)
    tables = [
        pltpu.make_async_copy(idt_hbm, idt_ref, sems.at[0]),
        pltpu.make_async_copy(id_hbm, id_ref, sems.at[1]),
    ]

    def take(i):
        at = pl.ds(i * GROUP, GROUP)
        return pltpu.make_async_copy(obs_hbm.at[at, rows_at, :], obs_ref.at[at], in_sems.at[i])

    def give(i):
        at = pl.ds(i * GROUP, GROUP)
        return pltpu.make_async_copy(resid_ref.at[at], resid_hbm.at[at], resid_sems.at[i])

    tables[0].start()
    take(0).start()
    tables[1].start()
    for i in range(1, groups):
        take(i).start()
    grad[...] = jnp.zeros_like(grad)
    for table in tables:
        table.wait()

    def step(i, _):
        take(i).wait()
        at = [(i * GROUP + u, slot_ref[i * GROUP + u], ident_ref[i * GROUP + u]) for u in range(GROUP)]
        scores = [jnp.dot(rows_ref[s], idt_ref[n], preferred_element_type=F32) for _, s, n in at]
        resids = []
        for (b, s, n), score in zip(at, scores):
            resid = (weight_ref[pl.ds(n, 1), :] * (score - obs_ref[b].astype(F32))).astype(BF16)
            resid_ref[b] = resid
            resids.append(resid)
        parts = [jnp.dot(resid, id_ref[n], preferred_element_type=F32) for resid, (_, _, n) in zip(resids, at)]
        for (_, s, _), part in zip(at, parts):
            grad[s] += part
        give(i).start()
        return 0

    lax.fori_loop(0, groups, step, 0)

    def fill(first, count):
        at = pl.ds(first, count)
        chunks[at] = grad[at].astype(BF16)

    store_parts(chunks, out_hbm, out_sems, fill)
    for i in range(groups):
        give(i).wait()


def ident_grad_kernel(
    core_ref,
    chip_ref,
    slot_ref,
    ident_ref,
    rows_ref,
    weight_ref,
    resid_hbm,
    keep_ref,
    send_ref,
    grad,
    turned,
    resid_ref,
    sems,
):
    blocks, half, _ = resid_ref.shape
    core = core_ref[0]

    def take(i):
        at = pl.ds(i * GROUP, GROUP)
        return pltpu.make_async_copy(resid_hbm.at[at], resid_ref.at[at], sems.at[i])

    for i in range(blocks // GROUP):
        take(i).start()
    grad[...] = jnp.zeros_like(grad)

    def turn(s, _):
        rows = rows_ref[s].astype(F32).T
        weight = weight_ref[pl.ds(combine(chip_ref[0], s, -1), 1), :half]
        turned[s] = (rows * weight).astype(BF16)
        return 0

    lax.fori_loop(0, rows_ref.shape[0], turn, 0, unroll=4)

    def step(i, _):
        take(i).wait()
        at = [(i * GROUP + u, slot_ref[i * GROUP + u], ident_ref[i * GROUP + u]) for u in range(GROUP)]
        parts = [jnp.dot(turned[s], resid_ref[b], preferred_element_type=F32) for b, s, _ in at]
        for (_, _, n), part in zip(at, parts):
            grad[n] += part
        return 0

    lax.fori_loop(0, blocks // GROUP, step, 0)
    own = pl.multiple_of(core * half, half)
    other = pl.multiple_of((1 - core) * half, half)
    for n in range(grad.shape[0]):
        keep_ref[n] = grad[n, pl.ds(own, half), :]
        send_ref[n] = grad[n, pl.ds(other, half), :]


def ident_update_kernel(id_ref, own_ref, peer_ref, out_ref):
    blk = own_ref.shape[2]
    for n in range(own_ref.shape[0]):
        old = id_ref[:, n * blk : (n + 1) * blk]
        grad = own_ref[n] + peer_ref[n]
        out_ref[:, n * blk : (n + 1) * blk] = old - STEP * (grad + DECAY * old)


def collect_kernel(core_ref, list_ref, back_ref, count_ref, keep_ref, send_ref, grad, weights):
    core = core_ref[0]
    pairs, half_cols, blk = keep_ref.shape
    half = blk // 2
    grad[...] = jnp.zeros_like(grad)
    weight = count_weight(count_ref[...]).astype(BF16).astype(F32)
    weights[...] = jnp.where(core == 0, weight, pltpu.roll(weight, half, 1))

    def add(e, _):
        r = list_ref[e]
        grad[r] += back_ref[e].astype(F32)
        return 0

    lax.fori_loop(0, back_ref.shape[0], add, 0, unroll=8)
    low = low_lanes(half)

    def pair(m, _):
        both = jnp.concatenate([grad[2 * m], grad[2 * m + 1]], axis=0).T
        row = jnp.where(low, weights[pl.ds(2 * m, 1), :], pltpu.roll(weights[pl.ds(2 * m + 1, 1), :], half, 1))
        both = both * row
        first, last = both[:half_cols], both[half_cols:]
        keep_ref[m] = jnp.where(core == 0, first, last)
        send_ref[m] = jnp.where(core == 0, last, first)
        return 0

    lax.fori_loop(0, pairs, pair, 0, unroll=2)


def record_update_kernel(core_ref, rec_ref, keep_ref, recv_ref, out_ref):
    core = core_ref[0]
    pairs, _, blk = keep_ref.shape
    low = low_lanes(blk // 2)

    def pair(m, _):
        keep, recv = keep_ref[m], recv_ref[m]
        half0 = jnp.where(core == 0, keep, recv)
        half1 = jnp.where(core == 0, recv, keep)
        grads = (
            jnp.where(low, half0, pltpu.roll(half1, blk // 2, 1)),
            jnp.where(low, pltpu.roll(half0, blk // 2, 1), half1),
        )
        for k, grad in enumerate(grads):
            at = pl.ds(pl.multiple_of(m * 2 * blk + k * blk, blk), blk)
            old = rec_ref[:, at]
            out_ref[:, at] = old - STEP * (grad + DECAY * old)
        return 0

    lax.fori_loop(0, pairs, pair, 0, unroll=2)


def call(kernel, outs, ins, scratch=(), sems=(), name=None):
    return pl.pallas_call(
        kernel,
        out_shape=[pltpu.HBM(o[0], o[1]) if len(o) > 2 else jax.ShapeDtypeStruct(*o) for o in outs],
        in_specs=ins,
        out_specs=[HBM if len(o) > 2 else VMEM for o in outs],
        scratch_shapes=[pltpu.VMEM(*t) for t in scratch] + [pltpu.SemaphoreType.DMA((n,)) for n in sems],
        compiler_params=PARAMS,
        name=name,
    )


def in_hbm(x):
    return pltpu.with_memory_space_constraint(x, pltpu.HBM)


def by_offsets(rows):
    width = rows.shape[1]
    chips = GRID[0] * GRID[1] * GRID[2]
    rows = rows.reshape(*GRID, width)
    for axis, extent in enumerate(GRID):
        stride = 1
        for n in GRID[axis + 1 :]:
            stride *= n
        parts = []
        for off in range(extent):
            part = lax.index_in_dim(rows, off, axis, keepdims=False)
            if off:
                pairs = []
                for g in range(chips):
                    at = (g // stride) % extent
                    pairs.append((g, g + ((at + off) % extent - at) * stride))
                part = lax.ppermute(part, "gx", pairs)
            parts.append(part)
        rows = jnp.stack(parts, axis)
    return rows.reshape(chips, width)


def body(records, idents, rec_count, id_count, observed, send_list, slot_of_block, id_of_block):
    peers = lax.axis_size("gx")
    core = lax.axis_index("gy").astype(jnp.int32).reshape(1)
    chip = lax.axis_index("gx").astype(jnp.int32).reshape(1)
    blocks, blk = observed.shape[0], observed.shape[1]
    half_cols = records.shape[1]
    rank = 2 * half_cols
    half = blk // 2
    recs, ids = records.shape[0] // blk, idents.shape[0] // blk
    pairs = recs // 2
    rec_t, id_t = records.T, idents.T
    sends = send_list.reshape(-1)
    rec_count, id_count = rec_count.reshape(recs, blk), id_count.reshape(ids, blk)
    swap = functools.partial(lax.ppermute, axis_name="gy", perm=[(0, 1), (1, 0)])
    exchange = functools.partial(lax.all_to_all, axis_name="gx", split_axis=0, concat_axis=0, tiled=True)

    half_shape = (pairs, half_cols, blk)
    chunk_shape = (peers, half, rank)
    keep, send = call(
        split_kernel, [(half_shape, BF16)] * 2, [SMEM, HBM], [(rec_t.shape, F32)], [4], name="split"
    )(core, in_hbm(rec_t))
    recv = swap(send)
    (chunks,) = call(
        pack_kernel,
        [(chunk_shape, BF16, True)],
        [SMEM, SMEM, VMEM, VMEM],
        [((recs, half, rank), BF16), (chunk_shape, BF16)],
        [4],
        name="pack",
    )(core, sends, keep, recv)
    arrived = exchange(chunks)

    (id_half,) = call(cast_kernel, [((ids, half_cols, blk), BF16)], [VMEM], name="cast")(id_t)
    id_peer = swap(id_half)
    idt, id_rows, id_weight = call(
        ident_kernel,
        [((ids, rank, blk), BF16), ((ids, blk, rank), BF16), ((ids, blk), F32)],
        [SMEM, VMEM, VMEM, VMEM],
        name="ident",
    )(core, id_half, id_peer, id_count)
    resid_shape = (blocks, half, blk)
    groups = blocks // GROUP
    resid, slot_grad = call(
        score_kernel,
        [(resid_shape, BF16, True), (chunk_shape, BF16, True)],
        [SMEM] * 3 + [VMEM] * 2 + [HBM] * 3,
        [
            ((ids, rank, blk), BF16),
            ((ids, blk, rank), BF16),
            (resid_shape, BF16),
            (resid_shape, BF16),
            (chunk_shape, F32),
            (chunk_shape, BF16),
        ],
        [2, groups, groups, 4],
        name="score",
    )(core, slot_of_block, id_of_block, arrived, id_weight, in_hbm(idt), in_hbm(id_rows), in_hbm(observed))
    returned = exchange(slot_grad)

    (weights,) = call(
        weigh_kernel, [((peers, blk), F32)], [SMEM, SMEM, SMEM, VMEM], [((recs, blk), F32)], name="weigh"
    )(core, chip, sends, rec_count)
    weights, resid = lax.optimization_barrier((weights, resid))
    arrived_weight = by_offsets(weights)
    id_keep, id_send = call(
        ident_grad_kernel,
        [((ids, half_cols, blk), F32)] * 2,
        [SMEM] * 4 + [VMEM] * 2 + [HBM],
        [((ids, rank, blk), F32), ((peers, rank, half), BF16), (resid_shape, BF16)],
        [groups],
        name="ident_grad",
    )(core, chip, slot_of_block, id_of_block, arrived, arrived_weight, in_hbm(resid))
    id_recv = swap(id_send)
    (new_id_t,) = call(ident_update_kernel, [(id_t.shape, F32)], [VMEM] * 3, name="ident_update")(
        id_t, id_keep, id_recv
    )

    rec_keep, rec_send = call(
        collect_kernel,
        [(half_shape, F32), (half_shape, F32)],
        [SMEM, SMEM, VMEM, VMEM],
        [((recs, half, rank), F32), ((recs, blk), F32)],
        name="collect",
    )(core, sends, returned, rec_count)
    rec_recv = swap(rec_send)
    (new_rec_t,) = call(record_update_kernel, [(rec_t.shape, F32)], [SMEM, VMEM, VMEM, VMEM], name="record_update")(
        core, rec_t, rec_keep, rec_recv
    )
    return new_rec_t.T, new_id_t.T


def solution(mesh):
    in_specs = (
        P("gx", "gy"),
        P("gx", "gy"),
        P("gx"),
        P("gx"),
        P("gx", None, None),
        P("gx", None),
        P("gx"),
        P("gx"),
    )
    out_specs = (P("gx", "gy"), P("gx", "gy"))
    return jax.shard_map(body, mesh=mesh, in_specs=in_specs, out_specs=out_specs, check_vma=False)
```

```python
import functools

import jax
import jax.numpy as jnp
from jax import lax
from jax.experimental import pallas as pl
from jax.experimental.pallas import tpu as pltpu
from jax.sharding import PartitionSpec as P

F32, BF16 = jnp.float32, jnp.bfloat16
STEP = 0.05
DECAY = 0.1
VMEM = pl.BlockSpec(memory_space=pltpu.VMEM)
SMEM = pl.BlockSpec(memory_space=pltpu.SMEM)
HBM = pl.BlockSpec(memory_space=pltpu.HBM)
GRID = (4, 8, 4)
PARAMS = pltpu.CompilerParams(vmem_limit_bytes=24 << 20)


def count_weight(count):
    return jnp.log(1.0 + count.astype(F32)) / jnp.log(F32(1001.0))


def low_lanes(half):
    lane = lax.broadcasted_iota(jnp.int32, (1, 2 * half), 1)
    return lane < half


def split_kernel(core_ref, rec_ref, keep_ref, send_ref, rows, sems):
    core = core_ref[0]
    pairs, _, blk = keep_ref.shape
    low = low_lanes(blk // 2)
    parts = sems.shape[0]
    width = rec_ref.shape[1] // parts

    def copy(p):
        at = pl.ds(p * width, width)
        return pltpu.make_async_copy(rec_ref.at[:, at], rows.at[:, at], sems.at[p])

    for p in range(parts):
        copy(p).start()
    for m in range(pairs):
        if m % (pairs // parts) == 0:
            copy(m // (pairs // parts)).wait()
        first = rows[:, 2 * m * blk : (2 * m + 1) * blk]
        second = rows[:, (2 * m + 1) * blk : (2 * m + 2) * blk]
        half0 = jnp.where(low, first, pltpu.roll(second, blk // 2, 1))
        half1 = jnp.where(low, pltpu.roll(first, blk // 2, 1), second)
        keep_ref[m] = jnp.where(core == 0, half0, half1).astype(BF16)
        send_ref[m] = jnp.where(core == 0, half1, half0).astype(BF16)


def cast_kernel(id_ref, out_ref):
    blk = out_ref.shape[2]
    for n in range(out_ref.shape[0]):
        out_ref[n] = id_ref[:, n * blk : (n + 1) * blk].astype(BF16)


def pack_kernel(core_ref, list_ref, keep_ref, recv_ref, out_ref, blocks, chunks, sems):
    core = core_ref[0]
    pairs, half_cols, blk = keep_ref.shape
    half = blk // 2

    def pair(m, _):
        keep, recv = keep_ref[m].astype(F32), recv_ref[m].astype(F32)
        low = jnp.where(core == 0, keep, recv)
        high = jnp.where(core == 0, recv, keep)
        rows = jnp.concatenate([low, high], axis=0).T.astype(BF16)
        blocks[2 * m] = rows[:half]
        blocks[2 * m + 1] = rows[half:]
        return 0

    lax.fori_loop(0, pairs, pair, 0, unroll=4)

    def chunk(e, _):
        chunks[e] = blocks[list_ref[e]]
        return 0

    store_parts(chunks, out_ref, sems, lambda first, count: lax.fori_loop(first, first + count, chunk, 0, unroll=8))


def store_parts(scratch, out_ref, sems, fill):
    parts = sems.shape[0]
    count = scratch.shape[0] // parts
    copies = []
    for p in range(parts):
        fill(p * count, count)
        at = pl.ds(p * count, count)
        copies.append(pltpu.make_async_copy(scratch.at[at], out_ref.at[at], sems.at[p]))
        copies[-1].start()
    for copy in copies:
        copy.wait()


def weigh_kernel(core_ref, chip_ref, list_ref, count_ref, out_ref, weights):
    core = core_ref[0]
    peers, blk = out_ref.shape
    weight = count_weight(count_ref[...]).astype(BF16).astype(F32)
    weights[...] = jnp.where(core == 0, weight, pltpu.roll(weight, blk // 2, 1))

    def row(d, _):
        out_ref[pl.ds(d, 1), :] = weights[pl.ds(list_ref[combine(chip_ref[0], d, 1)], 1), :]
        return 0

    lax.fori_loop(0, peers, row, 0, unroll=8)


def combine(chip, other, sign):
    result, shift = 0, 0
    for n in reversed(GRID):
        mask = (n - 1) << shift
        result = result | (((chip & mask) + sign * (other & mask)) & mask)
        shift += n.bit_length() - 1
    return result


def ident_kernel(core_ref, own_ref, peer_ref, count_ref, idt_ref, id_ref, weight_ref):
    core = core_ref[0]

    def block(n, _):
        own, peer = own_ref[n].astype(F32), peer_ref[n].astype(F32)
        low = jnp.where(core == 0, own, peer)
        high = jnp.where(core == 0, peer, own)
        full = jnp.concatenate([low, high], axis=0)
        idt_ref[n] = full.astype(BF16)
        id_ref[n] = full.T.astype(BF16)
        return 0

    lax.fori_loop(0, own_ref.shape[0], block, 0, unroll=2)
    weight_ref[...] = count_weight(count_ref[...])


GROUP = 48


def score_kernel(
    core_ref,
    slot_ref,
    ident_ref,
    rows_ref,
    weight_ref,
    idt_hbm,
    id_hbm,
    obs_hbm,
    resid_hbm,
    out_hbm,
    idt_ref,
    id_ref,
    obs_ref,
    resid_ref,
    grad,
    chunks,
    sems,
    in_sems,
    resid_sems,
    out_sems,
):
    blocks, half, _ = obs_ref.shape
    groups = blocks // GROUP
    rows_at = pl.ds(pl.multiple_of(core_ref[0] * half, half), half)
    tables = [
        pltpu.make_async_copy(idt_hbm, idt_ref, sems.at[0]),
        pltpu.make_async_copy(id_hbm, id_ref, sems.at[1]),
    ]

    def take(i):
        at = pl.ds(i * GROUP, GROUP)
        return pltpu.make_async_copy(obs_hbm.at[at, rows_at, :], obs_ref.at[at], in_sems.at[i])

    def give(i):
        at = pl.ds(i * GROUP, GROUP)
        return pltpu.make_async_copy(resid_ref.at[at], resid_hbm.at[at], resid_sems.at[i])

    tables[0].start()
    take(0).start()
    tables[1].start()
    for i in range(1, groups):
        take(i).start()
    grad[...] = jnp.zeros_like(grad)
    for table in tables:
        table.wait()

    def step(i, _):
        take(i).wait()
        at = [(i * GROUP + u, slot_ref[i * GROUP + u], ident_ref[i * GROUP + u]) for u in range(GROUP)]
        scores = [jnp.dot(rows_ref[s], idt_ref[n], preferred_element_type=F32) for _, s, n in at]
        resids = []
        for (b, s, n), score in zip(at, scores):
            resid = (weight_ref[pl.ds(n, 1), :] * (score - obs_ref[b].astype(F32))).astype(BF16)
            resid_ref[b] = resid
            resids.append(resid)
        parts = [jnp.dot(resid, id_ref[n], preferred_element_type=F32) for resid, (_, _, n) in zip(resids, at)]
        for (_, s, _), part in zip(at, parts):
            grad[s] += part
        give(i).start()
        return 0

    lax.fori_loop(0, groups, step, 0)

    def fill(first, count):
        at = pl.ds(first, count)
        chunks[at] = grad[at].astype(BF16)

    store_parts(chunks, out_hbm, out_sems, fill)
    for i in range(groups):
        give(i).wait()


def ident_grad_kernel(
    core_ref,
    chip_ref,
    slot_ref,
    ident_ref,
    rows_ref,
    weight_ref,
    resid_hbm,
    keep_ref,
    send_ref,
    grad,
    turned,
    resid_ref,
    sems,
):
    blocks, half, _ = resid_ref.shape
    core = core_ref[0]

    def take(i):
        at = pl.ds(i * GROUP, GROUP)
        return pltpu.make_async_copy(resid_hbm.at[at], resid_ref.at[at], sems.at[i])

    for i in range(blocks // GROUP):
        take(i).start()
    grad[...] = jnp.zeros_like(grad)

    def turn(s, _):
        rows = rows_ref[s].astype(F32).T
        weight = weight_ref[pl.ds(combine(chip_ref[0], s, -1), 1), :half]
        turned[s] = (rows * weight).astype(BF16)
        return 0

    lax.fori_loop(0, rows_ref.shape[0], turn, 0, unroll=4)

    def step(i, _):
        take(i).wait()
        at = [(i * GROUP + u, slot_ref[i * GROUP + u], ident_ref[i * GROUP + u]) for u in range(GROUP)]
        parts = [jnp.dot(turned[s], resid_ref[b], preferred_element_type=F32) for b, s, _ in at]
        for (_, _, n), part in zip(at, parts):
            grad[n] += part
        return 0

    lax.fori_loop(0, blocks // GROUP, step, 0)
    own = pl.multiple_of(core * half, half)
    other = pl.multiple_of((1 - core) * half, half)
    for n in range(grad.shape[0]):
        keep_ref[n] = grad[n, pl.ds(own, half), :]
        send_ref[n] = grad[n, pl.ds(other, half), :]


def ident_update_kernel(id_ref, own_ref, peer_ref, out_ref):
    blk = own_ref.shape[2]
    for n in range(own_ref.shape[0]):
        old = id_ref[:, n * blk : (n + 1) * blk]
        grad = own_ref[n] + peer_ref[n]
        out_ref[:, n * blk : (n + 1) * blk] = old - STEP * (grad + DECAY * old)


def collect_kernel(core_ref, list_ref, back_hbm, count_ref, keep_ref, send_ref, grad, weights, back_ref, sems):
    core = core_ref[0]
    pairs, half_cols, blk = keep_ref.shape
    half = blk // 2
    parts = sems.shape[0]
    count = back_ref.shape[0] // parts

    def take(p):
        at = pl.ds(p * count, count)
        return pltpu.make_async_copy(back_hbm.at[at], back_ref.at[at], sems.at[p])

    for p in range(parts):
        take(p).start()
    grad[...] = jnp.zeros_like(grad)
    weight = count_weight(count_ref[...]).astype(BF16).astype(F32)
    weights[...] = jnp.where(core == 0, weight, pltpu.roll(weight, half, 1))

    def add(e, _):
        grad[list_ref[e]] += back_ref[e].astype(F32)
        return 0

    for p in range(parts):
        take(p).wait()
        lax.fori_loop(p * count, (p + 1) * count, add, 0, unroll=8)
    low = low_lanes(half)

    def pair(m, _):
        both = jnp.concatenate([grad[2 * m], grad[2 * m + 1]], axis=0).T
        row = jnp.where(low, weights[pl.ds(2 * m, 1), :], pltpu.roll(weights[pl.ds(2 * m + 1, 1), :], half, 1))
        both = both * row
        first, last = both[:half_cols], both[half_cols:]
        keep_ref[m] = jnp.where(core == 0, first, last)
        send_ref[m] = jnp.where(core == 0, last, first)
        return 0

    lax.fori_loop(0, pairs, pair, 0, unroll=4)


def record_update_kernel(core_ref, rec_ref, keep_ref, recv_ref, out_hbm, out_ref, sems):
    core = core_ref[0]
    pairs, _, blk = keep_ref.shape
    low = low_lanes(blk // 2)
    parts = sems.shape[0]
    width = out_ref.shape[1] // parts
    copies = []
    for m in range(pairs):
        keep, recv = keep_ref[m], recv_ref[m]
        half0 = jnp.where(core == 0, keep, recv)
        half1 = jnp.where(core == 0, recv, keep)
        grads = (
            jnp.where(low, half0, pltpu.roll(half1, blk // 2, 1)),
            jnp.where(low, pltpu.roll(half0, blk // 2, 1), half1),
        )
        for k, grad in enumerate(grads):
            at = slice((2 * m + k) * blk, (2 * m + k + 1) * blk)
            old = rec_ref[:, at]
            out_ref[:, at] = old - STEP * (grad + DECAY * old)
        if (m + 1) % (pairs // parts) == 0:
            p = len(copies)
            at = pl.ds(p * width, width)
            copies.append(pltpu.make_async_copy(out_ref.at[:, at], out_hbm.at[:, at], sems.at[p]))
            copies[-1].start()
    for copy in copies:
        copy.wait()


def call(kernel, outs, ins, scratch=(), sems=(), name=None):
    return pl.pallas_call(
        kernel,
        out_shape=[pltpu.HBM(o[0], o[1]) if len(o) > 2 else jax.ShapeDtypeStruct(*o) for o in outs],
        in_specs=ins,
        out_specs=[HBM if len(o) > 2 else VMEM for o in outs],
        scratch_shapes=[pltpu.VMEM(*t) for t in scratch] + [pltpu.SemaphoreType.DMA((n,)) for n in sems],
        compiler_params=PARAMS,
        name=name,
    )


def in_hbm(x):
    return pltpu.with_memory_space_constraint(x, pltpu.HBM)


def by_offsets(rows):
    width = rows.shape[1]
    chips = GRID[0] * GRID[1] * GRID[2]
    rows = rows.reshape(*GRID, width)
    for axis in (0, 2, 1):
        extent = GRID[axis]
        stride = 1
        for n in GRID[axis + 1 :]:
            stride *= n
        parts = []
        for off in range(extent):
            part = lax.index_in_dim(rows, off, axis, keepdims=False)
            if off:
                pairs = []
                for g in range(chips):
                    at = (g // stride) % extent
                    pairs.append((g, g + ((at + off) % extent - at) * stride))
                part = lax.ppermute(part, "gx", pairs)
            parts.append(part)
        rows = jnp.stack(parts, axis)
    return rows.reshape(chips, width)


def body(records, idents, rec_count, id_count, observed, send_list, slot_of_block, id_of_block):
    peers = lax.axis_size("gx")
    core = lax.axis_index("gy").astype(jnp.int32).reshape(1)
    chip = lax.axis_index("gx").astype(jnp.int32).reshape(1)
    blocks, blk = observed.shape[0], observed.shape[1]
    half_cols = records.shape[1]
    rank = 2 * half_cols
    half = blk // 2
    recs, ids = records.shape[0] // blk, idents.shape[0] // blk
    pairs = recs // 2
    rec_t, id_t = records.T, idents.T
    sends = send_list.reshape(-1)
    rec_count, id_count = rec_count.reshape(recs, blk), id_count.reshape(ids, blk)
    swap = functools.partial(lax.ppermute, axis_name="gy", perm=[(0, 1), (1, 0)])
    exchange = functools.partial(lax.all_to_all, axis_name="gx", split_axis=0, concat_axis=0, tiled=True)

    half_shape = (pairs, half_cols, blk)
    chunk_shape = (peers, half, rank)
    keep, send = call(
        split_kernel, [(half_shape, BF16)] * 2, [SMEM, HBM], [(rec_t.shape, F32)], [4], name="split"
    )(core, in_hbm(rec_t))
    recv = swap(send)
    (chunks,) = call(
        pack_kernel,
        [(chunk_shape, BF16, True)],
        [SMEM, SMEM, VMEM, VMEM],
        [((recs, half, rank), BF16), (chunk_shape, BF16)],
        [4],
        name="pack",
    )(core, in_hbm(sends), keep, recv)
    late_count, chunks = lax.optimization_barrier((rec_count, chunks))
    arrived = exchange(chunks)
    (weights,) = call(
        weigh_kernel, [((peers, blk), F32)], [SMEM, SMEM, SMEM, VMEM], [((recs, blk), F32)], name="weigh"
    )(core, chip, sends, late_count)
    arrived_weight = by_offsets(weights)

    (id_half,) = call(cast_kernel, [((ids, half_cols, blk), BF16)], [VMEM], name="cast")(id_t)
    id_peer = swap(id_half)
    idt, id_rows, id_weight = call(
        ident_kernel,
        [((ids, rank, blk), BF16), ((ids, blk, rank), BF16), ((ids, blk), F32)],
        [SMEM, VMEM, VMEM, VMEM],
        name="ident",
    )(core, id_half, id_peer, id_count)
    arrived_weight, id_weight = lax.optimization_barrier((arrived_weight, id_weight))
    resid_shape = (blocks, half, blk)
    groups = blocks // GROUP
    resid, slot_grad = call(
        score_kernel,
        [(resid_shape, BF16, True), (chunk_shape, BF16, True)],
        [SMEM] * 3 + [VMEM] * 2 + [HBM] * 3,
        [
            ((ids, rank, blk), BF16),
            ((ids, blk, rank), BF16),
            (resid_shape, BF16),
            (resid_shape, BF16),
            (chunk_shape, F32),
            (chunk_shape, BF16),
        ],
        [2, groups, groups, 4],
        name="score",
    )(core, slot_of_block, id_of_block, arrived, id_weight, in_hbm(idt), in_hbm(id_rows), in_hbm(observed))
    returned = exchange(slot_grad)

    id_keep, id_send = call(
        ident_grad_kernel,
        [((ids, half_cols, blk), F32)] * 2,
        [SMEM] * 4 + [VMEM] * 2 + [HBM],
        [((ids, rank, blk), F32), ((peers, rank, half), BF16), (resid_shape, BF16)],
        [groups],
        name="ident_grad",
    )(core, chip, slot_of_block, id_of_block, arrived, arrived_weight, in_hbm(resid))
    id_recv = swap(id_send)
    (new_id_t,) = call(ident_update_kernel, [(id_t.shape, F32)], [VMEM] * 3, name="ident_update")(
        id_t, id_keep, id_recv
    )

    rec_keep, rec_send = call(
        collect_kernel,
        [(half_shape, F32), (half_shape, F32)],
        [SMEM, SMEM, HBM, VMEM],
        [((recs, half, rank), F32), ((recs, blk), F32), (chunk_shape, BF16)],
        [8],
        name="collect",
    )(core, sends, in_hbm(returned), rec_count)
    rec_recv = swap(rec_send)
    (new_rec_t,) = call(
        record_update_kernel,
        [(rec_t.shape, F32, True)],
        [SMEM, VMEM, VMEM, VMEM],
        [(rec_t.shape, F32)],
        [4],
        name="record_update",
    )(core, rec_t, rec_keep, rec_recv)
    return new_rec_t.T, new_id_t.T


def solution(mesh):
    in_specs = (
        P("gx", "gy"),
        P("gx", "gy"),
        P("gx"),
        P("gx"),
        P("gx", None, None),
        P("gx", None),
        P("gx"),
        P("gx"),
    )
    out_specs = (P("gx", "gy"), P("gx", "gy"))
    return jax.shard_map(body, mesh=mesh, in_specs=in_specs, out_specs=out_specs, check_vma=False)
```

```python
import functools

import jax
import jax.numpy as jnp
from jax import lax
from jax.experimental import pallas as pl
from jax.experimental.pallas import tpu as pltpu
from jax.sharding import PartitionSpec as P

F32, BF16 = jnp.float32, jnp.bfloat16
STEP = 0.05
DECAY = 0.1
VMEM = pl.BlockSpec(memory_space=pltpu.VMEM)
SMEM = pl.BlockSpec(memory_space=pltpu.SMEM)
HBM = pl.BlockSpec(memory_space=pltpu.HBM)
TILE = 8
PARAMS = pltpu.CompilerParams(vmem_limit_bytes=24 << 20)


def count_weight(count):
    return jnp.log(1.0 + count.astype(F32)) / jnp.log(F32(1001.0))


def low_lanes(half):
    lane = lax.broadcasted_iota(jnp.int32, (1, 2 * half), 1)
    return lane < half


def split_kernel(core_ref, rec_ref, keep_ref, send_ref, rows, sems):
    core = core_ref[0]
    pairs, _, blk = keep_ref.shape
    low = low_lanes(blk // 2)
    parts = sems.shape[0]
    width = rec_ref.shape[1] // parts

    def copy(p):
        at = pl.ds(p * width, width)
        return pltpu.make_async_copy(rec_ref.at[:, at], rows.at[:, at], sems.at[p])

    for p in range(parts):
        copy(p).start()
    for m in range(pairs):
        if m % (pairs // parts) == 0:
            copy(m // (pairs // parts)).wait()
        first = rows[:, 2 * m * blk : (2 * m + 1) * blk]
        second = rows[:, (2 * m + 1) * blk : (2 * m + 2) * blk]
        half0 = jnp.where(low, first, pltpu.roll(second, blk // 2, 1))
        half1 = jnp.where(low, pltpu.roll(first, blk // 2, 1), second)
        keep_ref[m] = jnp.where(core == 0, half0, half1).astype(BF16)
        send_ref[m] = jnp.where(core == 0, half1, half0).astype(BF16)


def cast_kernel(id_ref, out_ref):
    blk = out_ref.shape[2]
    for n in range(out_ref.shape[0]):
        out_ref[n] = id_ref[:, n * blk : (n + 1) * blk].astype(BF16)


def pack_kernel(core_ref, list_ref, keep_ref, recv_ref, count_ref, out_ref, blocks, chunks, weights, sems):
    core = core_ref[0]
    pairs, half_cols, blk = keep_ref.shape
    half = blk // 2
    weight = count_weight(count_ref[...])
    weights[...] = jnp.where(core == 0, weight, pltpu.roll(weight, half, 1))

    def pair(m, _):
        keep, recv = keep_ref[m].astype(F32), recv_ref[m].astype(F32)
        low = jnp.where(core == 0, keep, recv)
        high = jnp.where(core == 0, recv, keep)
        rows = jnp.concatenate([low, high], axis=0).T.astype(BF16)
        for k in range(2):
            blocks[2 * m + k, :half] = rows[k * half : (k + 1) * half]
            weight = jnp.broadcast_to(weights[pl.ds(2 * m + k, 1), :], (TILE, blk))
            blocks[2 * m + k, half:] = weight.astype(BF16)
        return 0

    lax.fori_loop(0, pairs, pair, 0, unroll=4)

    def chunk(e, _):
        chunks[e] = blocks[list_ref[e]]
        return 0

    store_parts(chunks, out_ref, sems, lambda first, count: lax.fori_loop(first, first + count, chunk, 0, unroll=8))


def store_parts(scratch, out_ref, sems, fill):
    parts = sems.shape[0]
    count = scratch.shape[0] // parts
    copies = []
    for p in range(parts):
        fill(p * count, count)
        at = pl.ds(p * count, count)
        copies.append(pltpu.make_async_copy(scratch.at[at], out_ref.at[at], sems.at[p]))
        copies[-1].start()
    for copy in copies:
        copy.wait()


def ident_kernel(core_ref, own_ref, peer_ref, count_ref, idt_ref, id_ref, weight_ref):
    core = core_ref[0]

    def block(n, _):
        own, peer = own_ref[n].astype(F32), peer_ref[n].astype(F32)
        low = jnp.where(core == 0, own, peer)
        high = jnp.where(core == 0, peer, own)
        full = jnp.concatenate([low, high], axis=0)
        idt_ref[n] = full.astype(BF16)
        id_ref[n] = full.T.astype(BF16)
        return 0

    lax.fori_loop(0, own_ref.shape[0], block, 0, unroll=2)
    weight_ref[...] = count_weight(count_ref[...])


GROUP = 48


def score_kernel(
    core_ref,
    slot_ref,
    ident_ref,
    rows_ref,
    weight_ref,
    idt_hbm,
    id_hbm,
    obs_hbm,
    resid_hbm,
    out_hbm,
    idt_ref,
    id_ref,
    obs_ref,
    resid_ref,
    grad,
    chunks,
    sems,
    in_sems,
    resid_sems,
    out_sems,
):
    blocks, half, _ = obs_ref.shape
    groups = blocks // GROUP
    rows_at = pl.ds(pl.multiple_of(core_ref[0] * half, half), half)
    tables = [
        pltpu.make_async_copy(idt_hbm, idt_ref, sems.at[0]),
        pltpu.make_async_copy(id_hbm, id_ref, sems.at[1]),
    ]

    def take(i):
        at = pl.ds(i * GROUP, GROUP)
        return pltpu.make_async_copy(obs_hbm.at[at, rows_at, :], obs_ref.at[at], in_sems.at[i])

    def give(i):
        at = pl.ds(i * GROUP, GROUP)
        return pltpu.make_async_copy(resid_ref.at[at], resid_hbm.at[at], resid_sems.at[i])

    tables[0].start()
    take(0).start()
    tables[1].start()
    for i in range(1, groups):
        take(i).start()
    grad[...] = jnp.zeros_like(grad)
    for table in tables:
        table.wait()

    def step(i, _):
        take(i).wait()
        at = [(i * GROUP + u, slot_ref[i * GROUP + u], ident_ref[i * GROUP + u]) for u in range(GROUP)]
        scores = [jnp.dot(rows_ref[s, :half], idt_ref[n], preferred_element_type=F32) for _, s, n in at]
        resids = []
        for (b, s, n), score in zip(at, scores):
            resid = (weight_ref[pl.ds(n, 1), :] * (score - obs_ref[b].astype(F32))).astype(BF16)
            resid_ref[b] = resid
            resids.append(resid)
        parts = [jnp.dot(resid, id_ref[n], preferred_element_type=F32) for resid, (_, _, n) in zip(resids, at)]
        for (_, s, _), part in zip(at, parts):
            grad[s] += part
        give(i).start()
        return 0

    lax.fori_loop(0, groups, step, 0)

    def fill(first, count):
        at = pl.ds(first, count)
        chunks[at] = grad[at].astype(BF16)

    store_parts(chunks, out_hbm, out_sems, fill)
    for i in range(groups):
        give(i).wait()


def ident_grad_kernel(
    core_ref,
    slot_ref,
    ident_ref,
    rows_ref,
    resid_hbm,
    keep_ref,
    send_ref,
    grad,
    turned,
    resid_ref,
    sems,
):
    blocks, half, _ = resid_ref.shape
    core = core_ref[0]

    def take(i):
        at = pl.ds(i * GROUP, GROUP)
        return pltpu.make_async_copy(resid_hbm.at[at], resid_ref.at[at], sems.at[i])

    for i in range(blocks // GROUP):
        take(i).start()
    grad[...] = jnp.zeros_like(grad)

    def turn(s, _):
        rows = rows_ref[s, :half].astype(F32).T
        weight = rows_ref[s, half:].astype(F32)[:1, :half]
        turned[s] = (rows * weight).astype(BF16)
        return 0

    lax.fori_loop(0, rows_ref.shape[0], turn, 0, unroll=4)

    def step(i, _):
        take(i).wait()
        at = [(i * GROUP + u, slot_ref[i * GROUP + u], ident_ref[i * GROUP + u]) for u in range(GROUP)]
        parts = [jnp.dot(turned[s], resid_ref[b], preferred_element_type=F32) for b, s, _ in at]
        for (_, _, n), part in zip(at, parts):
            grad[n] += part
        return 0

    lax.fori_loop(0, blocks // GROUP, step, 0)
    own = pl.multiple_of(core * half, half)
    other = pl.multiple_of((1 - core) * half, half)
    for n in range(grad.shape[0]):
        keep_ref[n] = grad[n, pl.ds(own, half), :]
        send_ref[n] = grad[n, pl.ds(other, half), :]


def ident_update_kernel(id_ref, own_ref, peer_ref, out_ref):
    blk = own_ref.shape[2]
    for n in range(own_ref.shape[0]):
        old = id_ref[:, n * blk : (n + 1) * blk]
        grad = own_ref[n] + peer_ref[n]
        out_ref[:, n * blk : (n + 1) * blk] = old - STEP * (grad + DECAY * old)


def collect_kernel(core_ref, list_ref, back_hbm, count_ref, keep_ref, send_ref, grad, weights, back_ref, sems):
    core = core_ref[0]
    pairs, half_cols, blk = keep_ref.shape
    half = blk // 2
    parts = sems.shape[0]
    count = back_ref.shape[0] // parts

    def take(p):
        at = pl.ds(p * count, count)
        return pltpu.make_async_copy(back_hbm.at[at], back_ref.at[at], sems.at[p])

    for p in range(parts):
        take(p).start()
    grad[...] = jnp.zeros_like(grad)
    weight = count_weight(count_ref[...]).astype(BF16).astype(F32)
    weights[...] = jnp.where(core == 0, weight, pltpu.roll(weight, half, 1))

    def add(e, _):
        grad[list_ref[e]] += back_ref[e].astype(F32)
        return 0

    for p in range(parts):
        take(p).wait()
        lax.fori_loop(p * count, (p + 1) * count, add, 0, unroll=8)
    low = low_lanes(half)

    def pair(m, _):
        both = jnp.concatenate([grad[2 * m], grad[2 * m + 1]], axis=0).T
        row = jnp.where(low, weights[pl.ds(2 * m, 1), :], pltpu.roll(weights[pl.ds(2 * m + 1, 1), :], half, 1))
        both = both * row
        first, last = both[:half_cols], both[half_cols:]
        keep_ref[m] = jnp.where(core == 0, first, last)
        send_ref[m] = jnp.where(core == 0, last, first)
        return 0

    lax.fori_loop(0, pairs, pair, 0, unroll=4)


def record_update_kernel(core_ref, rec_ref, keep_ref, recv_ref, out_hbm, out_ref, sems):
    core = core_ref[0]
    pairs, _, blk = keep_ref.shape
    low = low_lanes(blk // 2)
    parts = sems.shape[0]
    width = out_ref.shape[1] // parts
    copies = []
    for m in range(pairs):
        keep, recv = keep_ref[m], recv_ref[m]
        half0 = jnp.where(core == 0, keep, recv)
        half1 = jnp.where(core == 0, recv, keep)
        grads = (
            jnp.where(low, half0, pltpu.roll(half1, blk // 2, 1)),
            jnp.where(low, pltpu.roll(half0, blk // 2, 1), half1),
        )
        for k, grad in enumerate(grads):
            at = slice((2 * m + k) * blk, (2 * m + k + 1) * blk)
            old = rec_ref[:, at]
            out_ref[:, at] = old - STEP * (grad + DECAY * old)
        if (m + 1) % (pairs // parts) == 0:
            p = len(copies)
            at = pl.ds(p * width, width)
            copies.append(pltpu.make_async_copy(out_ref.at[:, at], out_hbm.at[:, at], sems.at[p]))
            copies[-1].start()
    for copy in copies:
        copy.wait()


def call(kernel, outs, ins, scratch=(), sems=(), name=None):
    return pl.pallas_call(
        kernel,
        out_shape=[pltpu.HBM(o[0], o[1]) if len(o) > 2 else jax.ShapeDtypeStruct(*o) for o in outs],
        in_specs=ins,
        out_specs=[HBM if len(o) > 2 else VMEM for o in outs],
        scratch_shapes=[pltpu.VMEM(*t) for t in scratch] + [pltpu.SemaphoreType.DMA((n,)) for n in sems],
        compiler_params=PARAMS,
        name=name,
    )


def in_hbm(x):
    return pltpu.with_memory_space_constraint(x, pltpu.HBM)


def body(records, idents, rec_count, id_count, observed, send_list, slot_of_block, id_of_block):
    peers = lax.axis_size("gx")
    core = lax.axis_index("gy").astype(jnp.int32).reshape(1)
    blocks, blk = observed.shape[0], observed.shape[1]
    half_cols = records.shape[1]
    rank = 2 * half_cols
    half = blk // 2
    recs, ids = records.shape[0] // blk, idents.shape[0] // blk
    pairs = recs // 2
    rec_t, id_t = records.T, idents.T
    sends = send_list.reshape(-1)
    rec_count, id_count = rec_count.reshape(recs, blk), id_count.reshape(ids, blk)
    swap = functools.partial(lax.ppermute, axis_name="gy", perm=[(0, 1), (1, 0)])
    exchange = functools.partial(lax.all_to_all, axis_name="gx", split_axis=0, concat_axis=0, tiled=True)

    half_shape = (pairs, half_cols, blk)
    chunk_shape = (peers, half, rank)
    sent_shape = (peers, half + TILE, rank)
    keep, send = call(
        split_kernel, [(half_shape, BF16)] * 2, [SMEM, HBM], [(rec_t.shape, F32)], [4], name="split"
    )(core, in_hbm(rec_t))
    recv = swap(send)
    (chunks,) = call(
        pack_kernel,
        [(sent_shape, BF16, True)],
        [SMEM, SMEM, VMEM, VMEM, VMEM],
        [((recs, half + TILE, rank), BF16), (sent_shape, BF16), ((recs, blk), F32)],
        [4],
        name="pack",
    )(core, in_hbm(sends), keep, recv, in_hbm(rec_count))
    arrived = exchange(chunks)

    (id_half,) = call(cast_kernel, [((ids, half_cols, blk), BF16)], [VMEM], name="cast")(id_t)
    id_peer = swap(id_half)
    idt, id_rows, id_weight = call(
        ident_kernel,
        [((ids, rank, blk), BF16), ((ids, blk, rank), BF16), ((ids, blk), F32)],
        [SMEM, VMEM, VMEM, VMEM],
        name="ident",
    )(core, id_half, id_peer, id_count)
    resid_shape = (blocks, half, blk)
    groups = blocks // GROUP
    resid, slot_grad = call(
        score_kernel,
        [(resid_shape, BF16, True), (chunk_shape, BF16, True)],
        [SMEM] * 3 + [VMEM] * 2 + [HBM] * 3,
        [
            ((ids, rank, blk), BF16),
            ((ids, blk, rank), BF16),
            (resid_shape, BF16),
            (resid_shape, BF16),
            (chunk_shape, F32),
            (chunk_shape, BF16),
        ],
        [2, groups, groups, 4],
        name="score",
    )(core, slot_of_block, id_of_block, arrived, id_weight, in_hbm(idt), in_hbm(id_rows), in_hbm(observed))
    returned = exchange(slot_grad)

    id_keep, id_send = call(
        ident_grad_kernel,
        [((ids, half_cols, blk), F32)] * 2,
        [SMEM] * 3 + [VMEM, HBM],
        [((ids, rank, blk), F32), ((peers, rank, half), BF16), (resid_shape, BF16)],
        [groups],
        name="ident_grad",
    )(core, slot_of_block, id_of_block, arrived, in_hbm(resid))
    id_recv = swap(id_send)
    (new_id_t,) = call(ident_update_kernel, [(id_t.shape, F32)], [VMEM] * 3, name="ident_update")(
        id_t, id_keep, id_recv
    )

    rec_keep, rec_send = call(
        collect_kernel,
        [(half_shape, F32), (half_shape, F32)],
        [SMEM, SMEM, HBM, VMEM],
        [((recs, half, rank), F32), ((recs, blk), F32), (chunk_shape, BF16)],
        [8],
        name="collect",
    )(core, sends, in_hbm(returned), rec_count)
    rec_recv = swap(rec_send)
    (new_rec_t,) = call(
        record_update_kernel,
        [(rec_t.shape, F32, True)],
        [SMEM, VMEM, VMEM, VMEM],
        [(rec_t.shape, F32)],
        [4],
        name="record_update",
    )(core, rec_t, rec_keep, rec_recv)
    return new_rec_t.T, new_id_t.T


def solution(mesh):
    in_specs = (
        P("gx", "gy"),
        P("gx", "gy"),
        P("gx"),
        P("gx"),
        P("gx", None, None),
        P("gx", None),
        P("gx"),
        P("gx"),
    )
    out_specs = (P("gx", "gy"), P("gx", "gy"))
    return jax.shard_map(body, mesh=mesh, in_specs=in_specs, out_specs=out_specs, check_vma=False)
```

```python
import functools

import jax
import jax.numpy as jnp
from jax import lax
from jax.experimental import pallas as pl
from jax.experimental.pallas import tpu as pltpu
from jax.sharding import PartitionSpec as P

F32, BF16 = jnp.float32, jnp.bfloat16
STEP = 0.05
DECAY = 0.1
VMEM = pl.BlockSpec(memory_space=pltpu.VMEM)
SMEM = pl.BlockSpec(memory_space=pltpu.SMEM)
HBM = pl.BlockSpec(memory_space=pltpu.HBM)
TILE = 8
PARAMS = pltpu.CompilerParams(vmem_limit_bytes=24 << 20)


def count_weight(count):
    return jnp.log(1.0 + count.astype(F32)) / jnp.log(F32(1001.0))


def low_lanes(half):
    lane = lax.broadcasted_iota(jnp.int32, (1, 2 * half), 1)
    return lane < half


def split_kernel(core_ref, rec_ref, keep_ref, send_ref, rows, sems):
    core = core_ref[0]
    pairs, _, blk = keep_ref.shape
    low = low_lanes(blk // 2)
    parts = sems.shape[0]
    width = rec_ref.shape[1] // parts

    def copy(p):
        at = pl.ds(p * width, width)
        return pltpu.make_async_copy(rec_ref.at[:, at], rows.at[:, at], sems.at[p])

    for p in range(parts):
        copy(p).start()
    for m in range(pairs):
        if m % (pairs // parts) == 0:
            copy(m // (pairs // parts)).wait()
        first = rows[:, 2 * m * blk : (2 * m + 1) * blk]
        second = rows[:, (2 * m + 1) * blk : (2 * m + 2) * blk]
        half0 = jnp.where(low, first, pltpu.roll(second, blk // 2, 1))
        half1 = jnp.where(low, pltpu.roll(first, blk // 2, 1), second)
        keep_ref[m] = jnp.where(core == 0, half0, half1).astype(BF16)
        send_ref[m] = jnp.where(core == 0, half1, half0).astype(BF16)


def cast_kernel(id_ref, out_ref):
    blk = out_ref.shape[2]
    for n in range(out_ref.shape[0]):
        out_ref[n] = id_ref[:, n * blk : (n + 1) * blk].astype(BF16)


def pack_kernel(core_ref, list_ref, keep_ref, recv_ref, count_ref, out_ref, blocks, chunks, weights, sems):
    core = core_ref[0]
    pairs, half_cols, blk = keep_ref.shape
    half = blk // 2
    weight = count_weight(count_ref[...])
    weights[...] = jnp.where(core == 0, weight, pltpu.roll(weight, half, 1))

    def pair(m, _):
        keep, recv = keep_ref[m].astype(F32), recv_ref[m].astype(F32)
        low = jnp.where(core == 0, keep, recv)
        high = jnp.where(core == 0, recv, keep)
        rows = jnp.concatenate([low, high], axis=0).T.astype(BF16)
        for k in range(2):
            blocks[2 * m + k, :half] = rows[k * half : (k + 1) * half]
            weight = jnp.broadcast_to(weights[pl.ds(2 * m + k, 1), :], (TILE, blk))
            blocks[2 * m + k, half:] = weight.astype(BF16)
        return 0

    lax.fori_loop(0, pairs, pair, 0, unroll=4)

    def chunk(e, _):
        chunks[e] = blocks[list_ref[e]]
        return 0

    store_parts(chunks, out_ref, sems, lambda first, count: lax.fori_loop(first, first + count, chunk, 0, unroll=8))


def store_parts(scratch, out_ref, sems, fill):
    parts = sems.shape[0]
    count = scratch.shape[0] // parts
    copies = []
    for p in range(parts):
        fill(p * count, count)
        at = pl.ds(p * count, count)
        copies.append(pltpu.make_async_copy(scratch.at[at], out_ref.at[at], sems.at[p]))
        copies[-1].start()
    for copy in copies:
        copy.wait()


def ident_kernel(core_ref, own_ref, peer_ref, count_ref, idt_ref, id_ref, weight_ref):
    core = core_ref[0]

    def block(n, _):
        own, peer = own_ref[n].astype(F32), peer_ref[n].astype(F32)
        low = jnp.where(core == 0, own, peer)
        high = jnp.where(core == 0, peer, own)
        full = jnp.concatenate([low, high], axis=0)
        idt_ref[n] = full.astype(BF16)
        id_ref[n] = full.T.astype(BF16)
        return 0

    lax.fori_loop(0, own_ref.shape[0], block, 0, unroll=2)
    weight_ref[...] = count_weight(count_ref[...])


SCORE_GROUP = 96
GROUP = 48


def score_kernel(
    core_ref,
    slot_ref,
    ident_ref,
    rows_ref,
    weight_ref,
    idt_hbm,
    id_hbm,
    obs_hbm,
    resid_hbm,
    out_hbm,
    idt_ref,
    id_ref,
    obs_ref,
    resid_ref,
    grad,
    chunks,
    sems,
    in_sems,
    resid_sems,
    out_sems,
):
    blocks, half, _ = obs_ref.shape
    groups = blocks // SCORE_GROUP
    rows_at = pl.ds(pl.multiple_of(core_ref[0] * half, half), half)
    tables = [
        pltpu.make_async_copy(idt_hbm, idt_ref, sems.at[0]),
        pltpu.make_async_copy(id_hbm, id_ref, sems.at[1]),
    ]

    def take(i):
        at = pl.ds(i * SCORE_GROUP, SCORE_GROUP)
        return pltpu.make_async_copy(obs_hbm.at[at, rows_at, :], obs_ref.at[at], in_sems.at[i])

    def give(i):
        at = pl.ds(i * SCORE_GROUP, SCORE_GROUP)
        return pltpu.make_async_copy(resid_ref.at[at], resid_hbm.at[at], resid_sems.at[i])

    tables[0].start()
    take(0).start()
    tables[1].start()
    for i in range(1, groups):
        take(i).start()
    grad[...] = jnp.zeros_like(grad)
    for table in tables:
        table.wait()

    def step(i, _):
        take(i).wait()
        at = [(i * SCORE_GROUP + u, slot_ref[i * SCORE_GROUP + u], ident_ref[i * SCORE_GROUP + u]) for u in range(SCORE_GROUP)]
        scores = [jnp.dot(rows_ref[s, :half], idt_ref[n], preferred_element_type=F32) for _, s, n in at]
        resids = []
        for (b, s, n), score in zip(at, scores):
            resid = (weight_ref[pl.ds(n, 1), :] * (score - obs_ref[b].astype(F32))).astype(BF16)
            resid_ref[b] = resid
            resids.append(resid)
        parts = [jnp.dot(resid, id_ref[n], preferred_element_type=F32) for resid, (_, _, n) in zip(resids, at)]
        for (_, s, _), part in zip(at, parts):
            grad[s] += part
        give(i).start()
        return 0

    lax.fori_loop(0, groups, step, 0)

    def fill(first, count):
        at = pl.ds(first, count)
        chunks[at] = grad[at].astype(BF16)

    store_parts(chunks, out_hbm, out_sems, fill)
    for i in range(groups):
        give(i).wait()


def ident_grad_kernel(
    core_ref,
    slot_ref,
    ident_ref,
    rows_ref,
    resid_hbm,
    keep_ref,
    send_ref,
    grad,
    turned,
    resid_ref,
    sems,
):
    blocks, half, _ = resid_ref.shape
    core = core_ref[0]

    def take(i):
        at = pl.ds(i * GROUP, GROUP)
        return pltpu.make_async_copy(resid_hbm.at[at], resid_ref.at[at], sems.at[i])

    for i in range(blocks // GROUP):
        take(i).start()
    grad[...] = jnp.zeros_like(grad)

    def turn(s, _):
        rows = rows_ref[s, :half].astype(F32).T
        weight = rows_ref[s, half:].astype(F32)[:1, :half]
        turned[s] = (rows * weight).astype(BF16)
        return 0

    lax.fori_loop(0, rows_ref.shape[0], turn, 0, unroll=4)

    def step(i, _):
        take(i).wait()
        at = [(i * GROUP + u, slot_ref[i * GROUP + u], ident_ref[i * GROUP + u]) for u in range(GROUP)]
        parts = [jnp.dot(turned[s], resid_ref[b], preferred_element_type=F32) for b, s, _ in at]
        for (_, _, n), part in zip(at, parts):
            grad[n] += part
        return 0

    lax.fori_loop(0, blocks // GROUP, step, 0)
    own = pl.multiple_of(core * half, half)
    other = pl.multiple_of((1 - core) * half, half)
    for n in range(grad.shape[0]):
        keep_ref[n] = grad[n, pl.ds(own, half), :]
        send_ref[n] = grad[n, pl.ds(other, half), :]


def ident_update_kernel(id_ref, own_ref, peer_ref, out_ref):
    blk = own_ref.shape[2]
    for n in range(own_ref.shape[0]):
        old = id_ref[:, n * blk : (n + 1) * blk]
        grad = own_ref[n] + peer_ref[n]
        out_ref[:, n * blk : (n + 1) * blk] = old - STEP * (grad + DECAY * old)


def collect_kernel(core_ref, list_ref, back_hbm, count_ref, keep_ref, send_ref, grad, weights, back_ref, sems):
    core = core_ref[0]
    pairs, half_cols, blk = keep_ref.shape
    half = blk // 2
    parts = sems.shape[0]
    count = back_ref.shape[0] // parts

    def take(p):
        at = pl.ds(p * count, count)
        return pltpu.make_async_copy(back_hbm.at[at], back_ref.at[at], sems.at[p])

    for p in range(parts):
        take(p).start()
    grad[...] = jnp.zeros_like(grad)
    weight = count_weight(count_ref[...]).astype(BF16).astype(F32)
    weights[...] = jnp.where(core == 0, weight, pltpu.roll(weight, half, 1))

    def add(e, _):
        grad[list_ref[e]] += back_ref[e].astype(F32)
        return 0

    for p in range(parts):
        take(p).wait()
        lax.fori_loop(p * count, (p + 1) * count, add, 0, unroll=8)
    low = low_lanes(half)

    def pair(m, _):
        both = jnp.concatenate([grad[2 * m], grad[2 * m + 1]], axis=0).T
        row = jnp.where(low, weights[pl.ds(2 * m, 1), :], pltpu.roll(weights[pl.ds(2 * m + 1, 1), :], half, 1))
        both = both * row
        first, last = both[:half_cols], both[half_cols:]
        keep_ref[m] = jnp.where(core == 0, first, last)
        send_ref[m] = jnp.where(core == 0, last, first).astype(BF16)
        return 0

    lax.fori_loop(0, pairs, pair, 0, unroll=4)


def record_update_kernel(core_ref, rec_ref, keep_ref, recv_ref, out_hbm, out_ref, sems):
    core = core_ref[0]
    pairs, _, blk = keep_ref.shape
    low = low_lanes(blk // 2)
    parts = sems.shape[0]
    width = out_ref.shape[1] // parts
    copies = []
    for m in range(pairs):
        keep, recv = keep_ref[m], recv_ref[m].astype(F32)
        half0 = jnp.where(core == 0, keep, recv)
        half1 = jnp.where(core == 0, recv, keep)
        grads = (
            jnp.where(low, half0, pltpu.roll(half1, blk // 2, 1)),
            jnp.where(low, pltpu.roll(half0, blk // 2, 1), half1),
        )
        for k, grad in enumerate(grads):
            at = slice((2 * m + k) * blk, (2 * m + k + 1) * blk)
            old = rec_ref[:, at]
            out_ref[:, at] = old - STEP * (grad + DECAY * old)
        if (m + 1) % (pairs // parts) == 0:
            p = len(copies)
            at = pl.ds(p * width, width)
            copies.append(pltpu.make_async_copy(out_ref.at[:, at], out_hbm.at[:, at], sems.at[p]))
            copies[-1].start()
    for copy in copies:
        copy.wait()


def call(kernel, outs, ins, scratch=(), sems=(), name=None):
    return pl.pallas_call(
        kernel,
        out_shape=[pltpu.HBM(o[0], o[1]) if len(o) > 2 else jax.ShapeDtypeStruct(*o) for o in outs],
        in_specs=ins,
        out_specs=[HBM if len(o) > 2 else VMEM for o in outs],
        scratch_shapes=[pltpu.VMEM(*t) for t in scratch] + [pltpu.SemaphoreType.DMA((n,)) for n in sems],
        compiler_params=PARAMS,
        name=name,
    )


def in_hbm(x):
    return pltpu.with_memory_space_constraint(x, pltpu.HBM)


def body(records, idents, rec_count, id_count, observed, send_list, slot_of_block, id_of_block):
    peers = lax.axis_size("gx")
    core = lax.axis_index("gy").astype(jnp.int32).reshape(1)
    blocks, blk = observed.shape[0], observed.shape[1]
    half_cols = records.shape[1]
    rank = 2 * half_cols
    half = blk // 2
    recs, ids = records.shape[0] // blk, idents.shape[0] // blk
    pairs = recs // 2
    rec_t, id_t = records.T, idents.T
    sends = send_list.reshape(-1)
    rec_count, id_count = rec_count.reshape(recs, blk), id_count.reshape(ids, blk)
    swap = functools.partial(lax.ppermute, axis_name="gy", perm=[(0, 1), (1, 0)])
    exchange = functools.partial(lax.all_to_all, axis_name="gx", split_axis=0, concat_axis=0, tiled=True)

    half_shape = (pairs, half_cols, blk)
    chunk_shape = (peers, half, rank)
    sent_shape = (peers, half + TILE, rank)
    keep, send = call(
        split_kernel, [(half_shape, BF16)] * 2, [SMEM, HBM], [(rec_t.shape, F32)], [4], name="split"
    )(core, in_hbm(rec_t))
    recv = swap(send)
    (chunks,) = call(
        pack_kernel,
        [(sent_shape, BF16, True)],
        [SMEM, SMEM, VMEM, VMEM, VMEM],
        [((recs, half + TILE, rank), BF16), (sent_shape, BF16), ((recs, blk), F32)],
        [4],
        name="pack",
    )(core, in_hbm(sends), keep, recv, in_hbm(rec_count))
    arrived = exchange(chunks)

    (id_half,) = call(cast_kernel, [((ids, half_cols, blk), BF16)], [VMEM], name="cast")(id_t)
    id_peer = swap(id_half)
    idt, id_rows, id_weight = call(
        ident_kernel,
        [((ids, rank, blk), BF16), ((ids, blk, rank), BF16), ((ids, blk), F32)],
        [SMEM, VMEM, VMEM, VMEM],
        name="ident",
    )(core, id_half, id_peer, id_count)
    resid_shape = (blocks, half, blk)
    groups = blocks // GROUP
    score_groups = blocks // SCORE_GROUP
    resid, slot_grad = call(
        score_kernel,
        [(resid_shape, BF16, True), (chunk_shape, BF16, True)],
        [SMEM] * 3 + [VMEM] * 2 + [HBM] * 3,
        [
            ((ids, rank, blk), BF16),
            ((ids, blk, rank), BF16),
            (resid_shape, BF16),
            (resid_shape, BF16),
            (chunk_shape, F32),
            (chunk_shape, BF16),
        ],
        [2, score_groups, score_groups, 4],
        name="score",
    )(core, slot_of_block, id_of_block, arrived, id_weight, in_hbm(idt), in_hbm(id_rows), in_hbm(observed))
    returned = exchange(slot_grad)

    id_keep, id_send = call(
        ident_grad_kernel,
        [((ids, half_cols, blk), F32)] * 2,
        [SMEM] * 3 + [VMEM, HBM],
        [((ids, rank, blk), F32), ((peers, rank, half), BF16), (resid_shape, BF16)],
        [groups],
        name="ident_grad",
    )(core, slot_of_block, id_of_block, arrived, in_hbm(resid))
    id_recv = swap(id_send)
    (new_id_t,) = call(ident_update_kernel, [(id_t.shape, F32)], [VMEM] * 3, name="ident_update")(
        id_t, id_keep, id_recv
    )

    rec_keep, rec_send = call(
        collect_kernel,
        [(half_shape, F32), (half_shape, BF16)],
        [SMEM, SMEM, HBM, VMEM],
        [((recs, half, rank), F32), ((recs, blk), F32), (chunk_shape, BF16)],
        [8],
        name="collect",
    )(core, sends, in_hbm(returned), rec_count)
    rec_recv = swap(rec_send)
    (new_rec_t,) = call(
        record_update_kernel,
        [(rec_t.shape, F32, True)],
        [SMEM, VMEM, VMEM, VMEM],
        [(rec_t.shape, F32)],
        [4],
        name="record_update",
    )(core, rec_t, rec_keep, rec_recv)
    return new_rec_t.T, new_id_t.T


def solution(mesh):
    in_specs = (
        P("gx", "gy"),
        P("gx", "gy"),
        P("gx"),
        P("gx"),
        P("gx", None, None),
        P("gx", None),
        P("gx"),
        P("gx"),
    )
    out_specs = (P("gx", "gy"), P("gx", "gy"))
    return jax.shard_map(body, mesh=mesh, in_specs=in_specs, out_specs=out_specs, check_vma=False)
```
